256 devices in a mesh: ctx: 32 (over y, x, core), head: 8 (over z).
Axes of the slice: x: 4, y: 4, z: 8, core: 2. Of those that a mesh axis runs over, the one named last changes fastest.
Arguments:
- queries: bfloat16 [32768, 2048], P(('ctx', 'head')), may hold values from -6 to 6
- keys: bfloat16 [32768, 2048], P(('ctx', 'head')), may hold values from -6 to 6
- values: bfloat16 [32768, 2048], P(('ctx', 'head')), may hold values from -6 to 6
- grad_out: bfloat16 [32768, 2048], P(('ctx', 'head')), may hold values from -6 to 6
- gain: float32 [2048], replicated, may hold values from 0.1 to 1.9
- lengths: int32 [4], replicated, may hold values from 1 to 16384, 32768 in all
- block_mask: int32 [64, 6], P('ctx'), may hold values 0 or 1
Outputs:
- output: bfloat16 [32768, 2048], P(('ctx', 'head'))
- grad_queries: bfloat16 [32768, 2048], P(('ctx', 'head'))
- grad_keys: bfloat16 [32768, 2048], P(('ctx', 'head'))
- grad_values: bfloat16 [32768, 2048], P(('ctx', 'head'))
The draws below stay inside these ranges and needn't reach their ends.
Inputs may be any that keep to these rules, and one draw needn't show every extreme that they name: The lengths of the 4 packed repertoires in order; they sum to 32768.
All inputs are finite; a program needn't handle non-finite values. No bound on the sum of `block_mask` on one device may be relied on, other than what follows from the above.
Results may differ from the reference program's by a relative error of at most 0.0051.
Values may be sent and summed in bfloat16 or wider, within the bound.
A program may use at most 64 MiB of HBM per device.

```python
import math
import jax
import jax.numpy as jnp
import numpy as np
from jax import lax

HEADS = 16
DH = 128
GROUP = 512
SEQS = 4
TOKENS = 32768


def with_ends(result, own_key, least, top_value):
    shape = result.shape
    spot = [jax.random.randint(jax.random.fold_in(own_key, axis), (), 0, shape[axis]) for axis in range(len(shape))]
    result = result.at[tuple(spot)].set(least)
    longest = shape.index(max(shape))
    spot[longest] = (spot[longest] + 1) % shape[longest]
    return result.at[tuple(spot)].set(top_value)


def block_scale(stream_key, shape, shards, least, high):
    level, own = 1.0, jax.random.fold_in(stream_key, 6)
    for axis_at, shards_of in shards:
        heights = jnp.exp(jax.random.uniform(jax.random.fold_in(own, axis_at), (shards_of,), jnp.float32, least / len(shards), high / len(shards)))
        level = level * jnp.repeat(heights, shape[axis_at] // shards_of).reshape([-1 if axis == axis_at else 1 for axis in range(len(shape))])
    return level


def profile(count, total, most, slope):
    portions = [(1 << 20) // math.isqrt(standing ** slope) + 1 for standing in range(2, count + 1)]
    rest, counts = total - most - (count - 1), [1] * (count - 1)
    while rest > 0:
        movable = [i for i in range(count - 1) if counts[i] < most]
        mass, remaining = sum([portions[i] for i in movable]), rest
        for i in movable:
            addition = min(most - counts[i], max(1, remaining * portions[i] // mass), rest)
            counts[i] = counts[i] + addition
            rest = rest - addition
    return np.array([most] + counts)


def uneven_parts(rng, number_of, total, reach, skew):
    if number_of == 2:
        one = jax.random.randint(rng, (), max(1, total - reach), min(reach, total - 1) + 1)
        return jnp.stack([one, total - one])
    sizes = jnp.asarray(profile(number_of, total, reach, skew), jnp.int32)
    couples = (number_of - 1) // 2
    source_of, receiver = sizes[1:1 + 2 * couples:2], sizes[2:2 + 2 * couples:2]
    margin = jnp.minimum(source_of - 1, reach - receiver)
    shifted = jax.random.randint(jax.random.fold_in(rng, 1), (couples,), 0, 1 << 20) % (margin + 1)
    sizes = sizes.at[1:1 + 2 * couples:2].set(source_of - shifted).at[2:2 + 2 * couples:2].set(receiver + shifted)
    return sizes[jax.random.permutation(jax.random.fold_in(rng, 2), number_of)]


def noise(own_key, shape, deviation, limit, pieces=(), kind=jnp.bfloat16):
    drawn = jax.random.normal(own_key, shape, jnp.float32) * deviation
    if len(pieces) > 0:
        drawn = block_scale(own_key, shape, pieces, -0.22, 0.18) * drawn
    return jnp.clip(drawn, min=-limit, max=limit).astype(kind)


def setup_inputs(seed: int = 0) -> dict:
    seeds = jax.random.split(jax.random.key(seed), 8)
    queries = noise(seeds[0], (TOKENS, HEADS * DH), 1.0, 6.0, ((0, 256),))
    keys = noise(seeds[1], (TOKENS, HEADS * DH), 1.0, 6.0, ((0, 256),))
    values = noise(seeds[2], (TOKENS, HEADS * DH), 1.0, 6.0, ((0, 256),))
    grad_out = noise(seeds[3], (TOKENS, HEADS * DH), 1.0, 6.0, ((0, 256),))
    gain = jnp.clip(1.0 + 0.18 * jax.random.normal(seeds[4], (HEADS * DH,), jnp.float32), 0.1, 1.9)
    lengths = uneven_parts(seeds[5], SEQS, TOKENS, TOKENS // 2, 2).astype(jnp.int32)
    block_mask = with_ends((jax.random.randint(seeds[6], (TOKENS // GROUP, 6), 0, 2) < 1).astype(jnp.int32), jax.random.fold_in(seeds[6], 1), 0, 1)
    return dict(queries=queries, keys=keys, values=values, grad_out=grad_out, gain=gain, lengths=lengths, block_mask=block_mask)


eps_norm = 1e-06
pair_slots = [-1, -1, -1, -1, 0, -1, -1, -1, 1, 2, -1, -1, 3, 4, 5, -1]

def segment_of(position, bounds):
    return lax.optimization_barrier(jnp.sum((position[..., None] >= bounds).astype(jnp.int32), axis=-1))

def group_weights(mask_row, seg_group):
    full_side = seg_group.shape[0]
    quarter = full_side // 4
    select = (lax.broadcasted_iota(jnp.int32, (6, 16), 0) == jnp.array(pair_slots, dtype=jnp.int32)[None, :]).astype(jnp.float32)
    blocks = jnp.dot(mask_row.astype(jnp.float32), select).reshape(4, 4) + jnp.eye(4, dtype=jnp.float32)
    spread = jnp.broadcast_to(blocks[:, None, :, None], (4, quarter, 4, quarter)).reshape(full_side, full_side)
    row_ids = lax.broadcasted_iota(jnp.int32, (full_side, full_side), 0)
    col_ids = lax.broadcasted_iota(jnp.int32, (full_side, full_side), 1)
    causal = (col_ids <= row_ids).astype(jnp.float32)
    shared = (seg_group[:, None] == seg_group[None, :]).astype(jnp.float32)
    return spread * causal * shared

def as_float(source):
    return source.astype(jnp.float32)

def reference(queries, keys, values, grad_out, gain, lengths, block_mask):
    tok_total, full_width = queries.shape
    head_count = full_width // DH
    group_count = tok_total // GROUP

    def blocked(source):
        return source.reshape(group_count, GROUP, head_count, DH)
    bounds = jnp.cumsum(lengths)[:3].astype(jnp.int32)
    positions = lax.iota(jnp.int32, tok_total).reshape(group_count, GROUP)
    seg_ids = segment_of(positions, bounds)
    seg_before = segment_of(positions[:, 0] - 1, bounds)
    seg_after = segment_of(positions[:, -1] + 1, bounds)
    seg_start = seg_ids[:, 0]
    seg_end = seg_ids[:, -1]
    q_blocks = blocked(queries)
    k_blocks = blocked(keys)
    v_blocks = blocked(values)
    highest = lax.Precision.HIGHEST

    def forward_step(kv_carry, inputs):
        q_part, k_part, v_part, mask_row, seg_group, before_seg, end_seg = inputs
        weights = group_weights(mask_row, seg_group)
        before_mask = (seg_group == before_seg).astype(jnp.float32)
        scores = jnp.einsum('thd,shd->hts', as_float(q_part), as_float(k_part)) * weights[None]
        prob_bf = scores.astype(jnp.bfloat16)
        intra_term = jnp.einsum('hts,shd->thd', as_float(prob_bf), as_float(v_part))
        inter_term = jnp.einsum('thi,hij->thj', as_float(q_part), kv_carry, precision=highest)
        raw_part = (intra_term + inter_term * before_mask[:, None, None]).astype(jnp.bfloat16)
        end_mask = (seg_group == end_seg).astype(jnp.float32)
        update = jnp.einsum('thi,thj->hij', as_float(k_part) * end_mask[:, None, None], as_float(v_part))
        carry_on = (end_seg == before_seg).astype(jnp.float32)
        return (carry_on * kv_carry + update, (raw_part, kv_carry))
    zero_state = jnp.zeros((head_count, DH, DH), jnp.float32)
    _, (raw_blocks, kv_states) = lax.scan(forward_step, zero_state, (q_blocks, k_blocks, v_blocks, block_mask, seg_ids, seg_before, seg_end))
    raw = raw_blocks.reshape(tok_total, full_width)
    raw_float = raw.astype(jnp.float32)
    scale_rms = jnp.sqrt(lax.optimization_barrier(jnp.sum(raw_float * raw_float, axis=1)) / full_width + eps_norm)
    normed = raw_float / scale_rms[:, None]
    output = (normed * gain[None, :]).astype(jnp.bfloat16)
    grad_norm = grad_out.astype(jnp.float32) * gain[None, :]
    cross_mean = lax.optimization_barrier(jnp.sum(grad_norm * normed, axis=1)) / full_width
    grad_raw = ((grad_norm - normed * cross_mean[:, None]) / scale_rms[:, None]).astype(jnp.bfloat16)
    d_blocks = blocked(grad_raw)

    def backward_step(grad_carry, inputs):
        q_part, k_part, v_part, d_part, mask_row, seg_group, before_seg, after_seg, start_seg, kv_state = inputs
        weights = group_weights(mask_row, seg_group)
        before_mask = (seg_group == before_seg).astype(jnp.float32)
        after_mask = (seg_group == after_seg).astype(jnp.float32)
        start_mask = (seg_group == start_seg).astype(jnp.float32)
        prob_bf = (jnp.einsum('thd,shd->hts', as_float(q_part), as_float(k_part)) * weights[None]).astype(jnp.bfloat16)
        grad_probs = (jnp.einsum('thd,shd->hts', as_float(d_part), as_float(v_part)) * weights[None]).astype(jnp.bfloat16)
        grad_q = jnp.einsum('hts,shd->thd', as_float(grad_probs), as_float(k_part)) + jnp.einsum('thj,hij->thi', as_float(d_part), kv_state, precision=highest) * before_mask[:, None, None]
        grad_k = jnp.einsum('hts,thd->shd', as_float(grad_probs), as_float(q_part)) + jnp.einsum('shj,hij->shi', as_float(v_part), grad_carry, precision=highest) * after_mask[:, None, None]
        grad_v = jnp.einsum('hts,thd->shd', as_float(prob_bf), as_float(d_part)) + jnp.einsum('shi,hij->shj', as_float(k_part), grad_carry, precision=highest) * after_mask[:, None, None]
        update = jnp.einsum('thi,thj->hij', as_float(q_part) * start_mask[:, None, None], as_float(d_part))
        carry_on = (start_seg == after_seg).astype(jnp.float32)
        outs_part = (grad_q.astype(jnp.bfloat16), grad_k.astype(jnp.bfloat16), grad_v.astype(jnp.bfloat16))
        return (carry_on * grad_carry + update, outs_part)
    _, (grad_qs, grad_ks, grad_vs) = lax.scan(backward_step, zero_state, (q_blocks, k_blocks, v_blocks, d_blocks, block_mask, seg_ids, seg_before, seg_after, seg_start, kv_states), reverse=True)
    return (output, grad_qs.reshape(tok_total, full_width), grad_ks.reshape(tok_total, full_width), grad_vs.reshape(tok_total, full_width))
```

```python
import jax
import jax.numpy as jnp
from jax import lax
from jax.experimental import pallas as pl
from jax.experimental.pallas import tpu as pltpu
from jax.sharding import Mesh
from jax.sharding import PartitionSpec as P

HEADS = 16
DH = 128
GROUP = 512
BLOCK = 128
EPS = 1e-06
F32 = jnp.float32
BF16 = jnp.bfloat16
TOKEN_AXES = ("cy", "cx", "cc", "head")
NY, NX, NC, NZ = 4, 4, 2, 8
CHIP = NC * NZ
MESH_ID = pl.DeviceIdType.MESH
CHUNKS = 2
ROWS = DH // CHUNKS


def mm(a, b, dims):
    return lax.dot_general(a, b, (dims, ((), ())), preferred_element_type=F32)


NN = ((1,), (0,))
NT = ((1,), (1,))
TN = ((0,), (0,))


def kernel(
    lengths, block_mask, q_ref, k_ref, v_ref, go_ref, gain_ref,
    out_ref, gq_ref, gk_ref, gv_ref,
    mask_mine, mask_all, probs, gprobs, diag, acc_k, acc_v, d_ref,
    m_loc, m_own, x_own, x_loc, n_loc, n_own, y_own, y_loc,
    tot_x, rec_x, tot_y, rec_y,
    a_send, a_recv, b_send, b_recv, x_send, x_recv, y_send, y_recv, mask_send, mask_recv,
):
    iy, ix, ic, iz = (lax.axis_index(a) for a in TOKEN_AXES)
    chip = iy * NX + ix
    mine = ic * NZ + iz
    owner = iz * NC + ic
    base = chip * (CHIP * BLOCK)
    start = base + mine * BLOCK

    barrier = pltpu.get_barrier_semaphore()

    def peer(step):
        e = lax.rem(owner + step, CHIP)
        return e, {"head": e // NC, "cc": lax.rem(e, NC)}

    def greet(step, carry):
        pl.semaphore_signal(barrier, 1, device_id=peer(step)[1], device_id_type=MESH_ID)
        return carry

    lax.fori_loop(1, CHIP, greet, 0)
    for step in range(1, NX):
        pl.semaphore_signal(
            barrier, 1, device_id={"cx": lax.rem(ix + step, NX)}, device_id_type=MESH_ID
        )
    for step in range(1, NY):
        pl.semaphore_signal(
            barrier, 1, device_id={"cy": lax.rem(iy + step, NY)}, device_id_type=MESH_ID
        )

    b1 = lengths[0]
    b2 = b1 + lengths[1]
    b3 = b2 + lengths[2]

    def seg(p):
        return (
            (p >= b1).astype(jnp.int32) + (p >= b2).astype(jnp.int32) + (p >= b3).astype(jnp.int32)
        )

    def same(a, b):
        return (a == b).astype(F32)

    for g in range(2):
        for n in range(6):
            mask_mine[8 * g + n : 8 * g + n + 1, :] = jnp.full(
                (1, DH), block_mask[g, n].astype(F32), F32
            )

    rows = lax.broadcasted_iota(jnp.int32, (BLOCK, BLOCK), 0)
    cols = lax.broadcasted_iota(jnp.int32, (BLOCK, BLOCK), 1)
    seg_r = seg(start + rows)
    seg_c = seg(start + cols)
    weight = jnp.where((seg_r == seg_c) & (cols <= rows), 1.0, 0.0).astype(F32)
    ends = jnp.where(seg_r == seg(start + BLOCK - 1), 1.0, 0.0).astype(BF16)
    starts = jnp.where(seg_r == seg(start), 1.0, 0.0).astype(BF16)
    before = jnp.where(seg_r == seg(start - 1), 1.0, 0.0).astype(BF16)
    after = jnp.where(seg_r == seg(start + BLOCK), 1.0, 0.0).astype(BF16)

    def col(h):
        return slice(h * DH, (h + 1) * DH)

    for h in range(HEADS):
        m_loc[h] = mm(k_ref[:, col(h)] * ends, v_ref[:, col(h)], TN).astype(BF16)

    pl.semaphore_wait(barrier, CHIP - 1 + NX - 1 + NY - 1)

    mask_copy = pltpu.make_async_remote_copy(
        src_ref=mask_mine,
        dst_ref=mask_all.at[ic],
        send_sem=mask_send,
        recv_sem=mask_recv,
        device_id={"cc": 1 - ic},
        device_id_type=MESH_ID,
    )
    mask_copy.start()
    mask_all[ic] = mask_mine[...]

    def chunk(c):
        return pl.ds(c * ROWS, ROWS)

    def scatter_copy(src, dst, c, step, phase):
        e, to = peer(step)
        return pltpu.make_async_remote_copy(
            src_ref=src.at[e, chunk(c)],
            dst_ref=dst.at[mine, chunk(c)],
            send_sem=a_send.at[phase, c, e],
            recv_sem=a_recv.at[phase, c, mine],
            device_id=to,
            device_id_type=MESH_ID,
        )

    def gather_copy(src, dst, c, step, phase):
        e, to = peer(step)
        r = lax.rem(e, NC) * NZ + e // NC
        return pltpu.make_async_remote_copy(
            src_ref=src.at[r, chunk(c)],
            dst_ref=dst.at[owner, chunk(c)],
            send_sem=b_send.at[phase, c, e],
            recv_sem=b_recv.at[phase, c, owner],
            device_id=to,
            device_id_type=MESH_ID,
        )

    def start_scatter(src, dst, phase):
        for c in range(CHUNKS):

            def go(step, carry):
                scatter_copy(src, dst, c, step, phase).start()
                return carry

            lax.fori_loop(1, CHIP, go, 0)
        dst[mine] = src[owner]

    def wait_scatter(src, dst, c, phase):
        def take(step, carry):
            e, to = peer(step)
            r = lax.rem(e, NC) * NZ + e // NC
            pltpu.make_async_remote_copy(
                src_ref=src.at[e, chunk(c)],
                dst_ref=dst.at[r, chunk(c)],
                send_sem=a_send.at[phase, c, e],
                recv_sem=a_recv.at[phase, c, r],
                device_id=to,
                device_id_type=MESH_ID,
            ).wait()
            return carry

        lax.fori_loop(1, CHIP, take, 0)

    def start_gather(src, dst, c, phase):
        def go(step, carry):
            gather_copy(src, dst, c, step, phase).start()
            return carry

        lax.fori_loop(1, CHIP, go, 0)
        dst[owner, chunk(c)] = src[mine, chunk(c)]

    def wait_gather(src, dst, c, phase):
        def take(step, carry):
            e, to = peer(step)
            r = lax.rem(e, NC) * NZ + e // NC
            pltpu.make_async_remote_copy(
                src_ref=src.at[r, chunk(c)],
                dst_ref=dst.at[e, chunk(c)],
                send_sem=b_send.at[phase, c, e],
                recv_sem=b_recv.at[phase, c, e],
                device_id=to,
                device_id_type=MESH_ID,
            ).wait()
            return carry

        lax.fori_loop(1, CHIP, take, 0)

    def line_copy(total, slots, c, phase, axis, me, to, slot, send, recv):
        return pltpu.make_async_remote_copy(
            src_ref=total.at[phase, chunk(c)],
            dst_ref=slots.at[phase, slot, chunk(c)],
            send_sem=send.at[phase, c, to],
            recv_sem=recv.at[phase, c, slot],
            device_id={axis: to},
            device_id_type=MESH_ID,
        )

    def exchange(total, slots, c, phase, axis, me, size, send, recv):
        for step in range(1, size):
            to = lax.rem(me + step, size)
            line_copy(total, slots, c, phase, axis, me, to, me, send, recv).start()
        slots[phase, me, chunk(c)] = total[phase, chunk(c)]
        for step in range(1, size):
            to = lax.rem(me + step, size)
            line_copy(total, slots, c, phase, axis, me, to, to, send, recv).wait()

    def states(own, result, c, phase):
        forward = phase == 0
        lo = [base + r * BLOCK for r in range(CHIP)]
        edge = [seg(p + BLOCK - 1) if forward else seg(p) for p in lo]
        want = [seg(p - 1) if forward else seg(p + BLOCK) for p in lo]
        last = CHIP - 1 if forward else 0
        chip_len = CHIP * BLOCK
        row_len = NX * chip_len
        row_at = iy * row_len
        enter = seg(base - 1) if forward else seg(base + chip_len)

        def edge_of(at, size):
            return seg(at + size - 1) if forward else seg(at)

        def block(r):
            return own[r, chunk(c)].astype(F32)

        total = block(last)
        for r in range(CHIP):
            if r != last:
                total += same(edge[r], edge[last]) * block(r)
        tot_x[phase, chunk(c)] = total
        exchange(tot_x, rec_x, c, phase, "cx", ix, NX, x_send, x_recv)
        row_edge = edge_of(row_at, row_len)
        row_total = jnp.zeros((ROWS, DH), F32)
        state = jnp.zeros((ROWS, DH), F32)
        for x in range(NX):
            part = rec_x[phase, x, chunk(c)]
            its = edge_of(row_at + x * chip_len, chip_len)
            row_total += same(its, row_edge) * part
            passed = (x < ix) if forward else (x > ix)
            state += same(its, enter) * passed.astype(F32) * part
        tot_y[phase, chunk(c)] = row_total
        exchange(tot_y, rec_y, c, phase, "cy", iy, NY, y_send, y_recv)
        for y in range(NY):
            its = edge_of(y * row_len, row_len)
            passed = (y < iy) if forward else (y > iy)
            state += same(its, enter) * passed.astype(F32) * rec_y[phase, y, chunk(c)]
        groups = range(CHIP // 4)
        reach = enter
        for g in groups if forward else reversed(groups):
            inner = range(4) if forward else (3, 2, 1, 0)
            seen = []
            for i in inner:
                r = 4 * g + i
                value = same(reach, want[r]) * state
                for j in seen:
                    hi, lo_ = (i, j) if forward else (j, i)
                    slot = 8 * (g % 2) + hi * (hi - 1) // 2 + lo_
                    pair = mask_all[g // 2, slot : slot + 1, :] * same(edge[4 * g + j], want[r])
                    value += pair * block(4 * g + j)
                result[r, chunk(c)] = value.astype(BF16)
                seen.append(i)
            far = 4 * g + (3 if forward else 0)
            state = same(reach, edge[far]) * state
            for i in inner:
                state += same(edge[4 * g + i], edge[far]) * block(4 * g + i)
            reach = edge[far]

    start_scatter(m_loc, m_own, 0)
    for h in range(HEADS):
        p = (mm(q_ref[:, col(h)], k_ref[:, col(h)], NT) * weight).astype(BF16)
        probs[h] = p
        diag[:, col(h)] = mm(p, v_ref[:, col(h)], NN)
    mask_copy.wait()
    for c in range(CHUNKS):
        wait_scatter(m_loc, m_own, c, 0)
        states(m_own, x_own, c, 0)
        start_gather(x_own, x_loc, c, 0)
    for c in range(CHUNKS):
        wait_gather(x_own, x_loc, c, 0)

    total_sq = jnp.zeros((BLOCK, DH), F32)
    total_gr = jnp.zeros((BLOCK, DH), F32)
    for h in range(HEADS):
        raw = (
            diag[:, col(h)] + mm(q_ref[:, col(h)] * before, x_loc[h], NN)
        ).astype(BF16).astype(F32)
        diag[:, col(h)] = raw
        scaled = go_ref[:, col(h)].astype(F32) * gain_ref[:, col(h)]
        total_sq += raw * raw
        total_gr += scaled * raw
    width = HEADS * DH
    inv = 1.0 / jnp.sqrt(jnp.sum(total_sq, axis=1, keepdims=True) / width + EPS)
    cross = jnp.sum(total_gr, axis=1, keepdims=True) * inv / width
    for h in range(HEADS):
        normed = diag[:, col(h)] * inv
        scaled = go_ref[:, col(h)].astype(F32) * gain_ref[:, col(h)]
        out_ref[:, col(h)] = (normed * gain_ref[:, col(h)]).astype(BF16)
        d = ((scaled - normed * cross) * inv).astype(BF16)
        d_ref[:, col(h)] = d
        n_loc[h] = mm(q_ref[:, col(h)] * starts, d, TN).astype(BF16)
    start_scatter(n_loc, n_own, 1)

    for h in range(HEADS):
        d = d_ref[:, col(h)]
        gp = (mm(d, v_ref[:, col(h)], NT) * weight).astype(BF16)
        gq_ref[:, col(h)] = (
            mm(gp, k_ref[:, col(h)], NN) + mm(d * before, x_loc[h], NT)
        ).astype(BF16)
        acc_k[:, col(h)] = mm(gp, q_ref[:, col(h)], TN)
        acc_v[:, col(h)] = mm(probs[h], d, TN)
    for c in range(CHUNKS):
        wait_scatter(n_loc, n_own, c, 1)
        states(n_own, y_own, c, 1)
        start_gather(y_own, y_loc, c, 1)
    for c in range(CHUNKS):
        wait_gather(y_own, y_loc, c, 1)
    for h in range(HEADS):
        y = y_loc[h]
        gk_ref[:, col(h)] = (acc_k[:, col(h)] + mm(v_ref[:, col(h)] * after, y, NT)).astype(BF16)
        gv_ref[:, col(h)] = (acc_v[:, col(h)] + mm(k_ref[:, col(h)] * after, y, NN)).astype(BF16)


def local(queries, keys, values, grad_out, gain, lengths, block_mask):
    shape = queries.shape
    vmem = pl.BlockSpec(memory_space=pltpu.VMEM)
    smem = pl.BlockSpec(memory_space=pltpu.SMEM)
    square = (HEADS, DH, DH)
    dma = pltpu.SemaphoreType.DMA
    return pl.pallas_call(
        kernel,
        out_shape=[jax.ShapeDtypeStruct(shape, BF16)] * 4,
        in_specs=[smem, smem, vmem, vmem, vmem, vmem, vmem],
        out_specs=[vmem] * 4,
        scratch_shapes=[
            pltpu.VMEM((16, DH), F32),
            pltpu.VMEM((2, 16, DH), F32),
            pltpu.VMEM(square, BF16),
            pltpu.VMEM((8, DH), BF16),
            pltpu.VMEM(shape, F32),
            pltpu.VMEM(shape, F32),
            pltpu.VMEM(shape, F32),
            pltpu.VMEM(shape, BF16),
        ]
        + [pltpu.VMEM(square, BF16)] * 8
        + [
            pltpu.VMEM((2, DH, DH), F32),
            pltpu.VMEM((2, NX, DH, DH), F32),
            pltpu.VMEM((2, DH, DH), F32),
            pltpu.VMEM((2, NY, DH, DH), F32),
            dma((2, CHUNKS, CHIP)),
            dma((2, CHUNKS, CHIP)),
            dma((2, CHUNKS, CHIP)),
            dma((2, CHUNKS, CHIP)),
            dma((2, CHUNKS, NX)),
            dma((2, CHUNKS, NX)),
            dma((2, CHUNKS, NY)),
            dma((2, CHUNKS, NY)),
            dma,
            dma,
        ],
        compiler_params=pltpu.CompilerParams(
            collective_id=0, has_side_effects=True, vmem_limit_bytes=40 * 1024 * 1024
        ),
    )(lengths, block_mask, queries, keys, values, grad_out, gain.reshape(1, -1))


def solution(mesh):
    torus = Mesh(mesh.devices.reshape(NY, NX, NC, NZ), TOKEN_AXES)
    tokens = P(TOKEN_AXES, None)
    in_specs = (tokens,) * 4 + (P(), P(), P(TOKEN_AXES[:3], None))
    return jax.shard_map(
        local, mesh=torus, in_specs=in_specs, out_specs=(tokens,) * 4, check_vma=False
    )
```

```python
import jax
import jax.numpy as jnp
from jax import lax
from jax.experimental import pallas as pl
from jax.experimental.pallas import tpu as pltpu
from jax.sharding import Mesh
from jax.sharding import PartitionSpec as P

HEADS = 16
DH = 128
GROUP = 512
BLOCK = 128
EPS = 1e-06
F32 = jnp.float32
BF16 = jnp.bfloat16
TOKEN_AXES = ("cy", "cx", "cc", "head")
NY, NX, NC, NZ = 4, 4, 2, 8
CHIP = NC * NZ
MESH_ID = pl.DeviceIdType.MESH
CHUNKS = 4
FAR_FIRST = True
SKEW = True
ROWS = DH // CHUNKS


def mm(a, b, dims):
    return lax.dot_general(a, b, (dims, ((), ())), preferred_element_type=F32)


NN = ((1,), (0,))
NT = ((1,), (1,))
TN = ((0,), (0,))


def kernel(
    lengths_hbm, mask_hbm, q_hbm, k_hbm, v_hbm, go_hbm, gain_hbm,
    out_ref, gq_ref, gk_ref, gv_ref,
    lengths, block_mask, q_ref, k_ref, v_ref, go_ref, gain_ref, in_sems,
    mask_mine, mask_all, probs, gprobs, diag, acc_k, acc_v, d_ref,
    m_loc, m_own, x_own, x_loc, n_loc, n_own, y_own, y_loc,
    tot_x, rec_x, tot_y, rec_y, entering,
    a_send, a_recv, b_send, b_recv, x_send, x_recv, y_send, y_recv, mask_send, mask_recv,
):
    iy, ix, ic, iz = (lax.axis_index(a) for a in TOKEN_AXES)
    chip = iy * NX + ix
    mine = ic * NZ + iz
    owner = iz * NC + ic
    base = chip * (CHIP * BLOCK)
    start = base + mine * BLOCK

    loads = [
        pltpu.make_async_copy(src, dst, in_sems.at[n])
        for n, (src, dst) in enumerate(
            (
                (lengths_hbm, lengths),
                (mask_hbm, block_mask),
                (k_hbm, k_ref),
                (v_hbm, v_ref),
                (q_hbm, q_ref),
                (gain_hbm, gain_ref),
                (go_hbm, go_ref),
            )
        )
    ]
    for load in loads:
        load.start()

    barrier = pltpu.get_barrier_semaphore()

    def peer(step):
        turn = (CHIP - step if FAR_FIRST else step)
        pair = turn // NC
        away = (pair + 1) // 2
        z = lax.rem(iz + jnp.where(lax.rem(pair, 2) == 1, away, NZ - away), NZ)
        c = lax.rem(ic + turn, NC)
        return z * NC + c, {"head": z, "cc": c}

    def greet(step, carry):
        pl.semaphore_signal(barrier, 1, device_id=peer(step)[1], device_id_type=MESH_ID)
        return carry

    lax.fori_loop(1, CHIP, greet, 0)
    for step in range(1, NX):
        pl.semaphore_signal(
            barrier, 1, device_id={"cx": lax.rem(ix + step, NX)}, device_id_type=MESH_ID
        )
    for step in range(1, NY):
        pl.semaphore_signal(
            barrier, 1, device_id={"cy": lax.rem(iy + step, NY)}, device_id_type=MESH_ID
        )

    loads[0].wait()
    loads[1].wait()
    b1 = lengths[0]
    b2 = b1 + lengths[1]
    b3 = b2 + lengths[2]

    def seg(p):
        return (
            (p >= b1).astype(jnp.int32) + (p >= b2).astype(jnp.int32) + (p >= b3).astype(jnp.int32)
        )

    def same(a, b):
        return (a == b).astype(F32)

    for g in range(2):
        for n in range(6):
            mask_mine[8 * g + n : 8 * g + n + 1, :] = jnp.full(
                (1, DH), block_mask[g, n].astype(F32), F32
            )

    rows = lax.broadcasted_iota(jnp.int32, (BLOCK, BLOCK), 0)
    cols = lax.broadcasted_iota(jnp.int32, (BLOCK, BLOCK), 1)
    seg_r = seg(start + rows)
    seg_c = seg(start + cols)
    weight = jnp.where((seg_r == seg_c) & (cols <= rows), 1.0, 0.0).astype(F32)
    ends = jnp.where(seg_r == seg(start + BLOCK - 1), 1.0, 0.0).astype(BF16)
    starts = jnp.where(seg_r == seg(start), 1.0, 0.0).astype(BF16)
    before = jnp.where(seg_r == seg(start - 1), 1.0, 0.0).astype(BF16)
    after = jnp.where(seg_r == seg(start + BLOCK), 1.0, 0.0).astype(BF16)

    def col(h):
        return slice(h * DH, (h + 1) * DH)

    with jax.named_scope("load_kv"):
        loads[2].wait()
        loads[3].wait()
    with jax.named_scope("make_m"):
        for h in range(HEADS):
            m_loc[h] = mm(k_ref[:, col(h)] * ends, v_ref[:, col(h)], TN).astype(BF16)

    with jax.named_scope("barrier"):
        pl.semaphore_wait(barrier, CHIP - 1 + NX - 1 + NY - 1)

    mask_copy = pltpu.make_async_remote_copy(
        src_ref=mask_mine,
        dst_ref=mask_all.at[ic],
        send_sem=mask_send,
        recv_sem=mask_recv,
        device_id={"cc": 1 - ic},
        device_id_type=MESH_ID,
    )
    mask_copy.start()
    mask_all[ic] = mask_mine[...]

    def chunk(c):
        return pl.ds(c * ROWS, ROWS)

    def scatter_copy(src, dst, c, step, phase):
        e, to = peer(step)
        return pltpu.make_async_remote_copy(
            src_ref=src.at[e, chunk(c)],
            dst_ref=dst.at[mine, chunk(c)],
            send_sem=a_send.at[phase, c],
            recv_sem=a_recv.at[phase, c],
            device_id=to,
            device_id_type=MESH_ID,
        )

    def gather_copy(src, dst, c, step, phase):
        e, to = peer(step)
        r = lax.rem(e, NC) * NZ + e // NC
        return pltpu.make_async_remote_copy(
            src_ref=src.at[r, chunk(c)],
            dst_ref=dst.at[owner, chunk(c)],
            send_sem=b_send.at[phase, c],
            recv_sem=b_recv.at[phase, c],
            device_id=to,
            device_id_type=MESH_ID,
        )

    def start_scatter(src, dst, phase):
        for c in range(CHUNKS):

            def go(step, carry):
                scatter_copy(src, dst, c, step, phase).start()
                return carry

            lax.fori_loop(1, CHIP, go, 0)
        dst[mine] = src[owner]

    others = pl.ds(0, CHIP - 1)

    def wait_square(src, dst, c, phase, send, recv):
        pltpu.make_async_remote_copy(
            src_ref=src.at[others, chunk(c)],
            dst_ref=dst.at[others, chunk(c)],
            send_sem=send.at[phase, c],
            recv_sem=recv.at[phase, c],
            device_id=peer(1)[1],
            device_id_type=MESH_ID,
        ).wait()

    def start_gather(src, dst, c, phase):
        def go(step, carry):
            gather_copy(src, dst, c, step, phase).start()
            return carry

        lax.fori_loop(1, CHIP, go, 0)
        dst[owner, chunk(c)] = src[mine, chunk(c)]

    def send_line(total, slots, c, phase, axis, me, size, send, recv):
        for step in range(1, size):
            pltpu.make_async_remote_copy(
                src_ref=total.at[phase, chunk(c)],
                dst_ref=slots.at[phase, me, chunk(c)],
                send_sem=send.at[phase, c],
                recv_sem=recv.at[phase, c],
                device_id={axis: lax.rem(me + (size - step if FAR_FIRST else step), size)},
                device_id_type=MESH_ID,
            ).start()
        slots[phase, me, chunk(c)] = total[phase, chunk(c)]

    def wait_line(slots, c, phase, axis, me, size, send, recv):
        rest = slots.at[phase, pl.ds(0, size - 1), chunk(c)]
        pltpu.make_async_remote_copy(
            src_ref=rest,
            dst_ref=rest,
            send_sem=send.at[phase, c],
            recv_sem=recv.at[phase, c],
            device_id={axis: lax.rem(me + 1, size)},
            device_id_type=MESH_ID,
        ).wait()

    chip_len = CHIP * BLOCK
    row_len = NX * chip_len
    row_at = iy * row_len
    along_x = ("cx", ix, NX, x_send, x_recv)
    along_y = ("cy", iy, NY, y_send, y_recv)

    def marks(phase):
        forward = phase == 0
        lo = [base + r * BLOCK for r in range(CHIP)]
        edge = [seg(p + BLOCK - 1) if forward else seg(p) for p in lo]
        want = [seg(p - 1) if forward else seg(p + BLOCK) for p in lo]
        enter = seg(base - 1) if forward else seg(base + chip_len)
        return forward, edge, want, enter

    def edge_of(forward, at, size):
        return seg(at + size - 1) if forward else seg(at)

    def stage_x(own, c, phase):
        forward, edge, _, _ = marks(phase)
        last = CHIP - 1 if forward else 0
        total = own[last, chunk(c)].astype(F32)
        for r in range(CHIP):
            if r != last:
                total += same(edge[r], edge[last]) * own[r, chunk(c)].astype(F32)
        tot_x[phase, chunk(c)] = total
        send_line(tot_x, rec_x, c, phase, *along_x)

    def stage_y(c, phase):
        forward, _, _, enter = marks(phase)
        wait_line(rec_x, c, phase, *along_x)
        row_edge = edge_of(forward, row_at, row_len)
        row_total = jnp.zeros((ROWS, DH), F32)
        partial = jnp.zeros((ROWS, DH), F32)
        for x in range(NX):
            part = rec_x[phase, x, chunk(c)]
            its = edge_of(forward, row_at + x * chip_len, chip_len)
            row_total += same(its, row_edge) * part
            passed = (x < ix) if forward else (x > ix)
            partial += same(its, enter) * passed.astype(F32) * part
        tot_y[phase, chunk(c)] = row_total
        send_line(tot_y, rec_y, c, phase, *along_y)
        entering[phase, chunk(c)] = partial

    def stage_out(own, result, c, phase):
        forward, edge, want, enter = marks(phase)
        wait_line(rec_y, c, phase, *along_y)
        state = entering[phase, chunk(c)]
        for y in range(NY):
            its = edge_of(forward, y * row_len, row_len)
            passed = (y < iy) if forward else (y > iy)
            state += same(its, enter) * passed.astype(F32) * rec_y[phase, y, chunk(c)]

        def block(r):
            return own[r, chunk(c)].astype(F32)

        groups = range(CHIP // 4)
        reach = enter
        for g in groups if forward else reversed(groups):
            inner = range(4) if forward else (3, 2, 1, 0)
            seen = []
            for i in inner:
                r = 4 * g + i
                value = same(reach, want[r]) * state
                for j in seen:
                    hi, lo = (i, j) if forward else (j, i)
                    slot = 8 * (g % 2) + hi * (hi - 1) // 2 + lo
                    pair = mask_all[g // 2, slot : slot + 1, :] * same(edge[4 * g + j], want[r])
                    value += pair * block(4 * g + j)
                result[r, chunk(c)] = value.astype(BF16)
                seen.append(i)
            far = 4 * g + (3 if forward else 0)
            state = same(reach, edge[far]) * state
            for i in inner:
                state += same(edge[4 * g + i], edge[far]) * block(4 * g + i)
            reach = edge[far]

    def spread(loc, own, result, back, phase):
        def first(c):
            with jax.named_scope("wait_scatter"):
                wait_square(loc, own, c, phase, a_send, a_recv)
            with jax.named_scope("stage_x"):
                stage_x(own, c, phase)

        def second(c):
            with jax.named_scope("stage_y"):
                stage_y(c, phase)

        def third(c):
            with jax.named_scope("stage_out"):
                stage_out(own, result, c, phase)
            with jax.named_scope("start_gather"):
                start_gather(result, back, c, phase)

        if SKEW:
            for s in range(CHUNKS + 2):
                if s < CHUNKS:
                    first(s)
                if 0 <= s - 1 < CHUNKS:
                    second(s - 1)
                if 0 <= s - 2 < CHUNKS:
                    third(s - 2)
        else:
            for s in range(CHUNKS):
                first(s)
                second(s)
                third(s)
        for c in range(CHUNKS):
            with jax.named_scope("wait_gather"):
                wait_square(result, back, c, phase, b_send, b_recv)

    with jax.named_scope("start_scatter"):
        start_scatter(m_loc, m_own, 0)
    for load in loads[4:]:
        load.wait()
    with jax.named_scope("diag"):
        for h in range(HEADS):
            p = (mm(q_ref[:, col(h)], k_ref[:, col(h)], NT) * weight).astype(BF16)
            probs[h] = p
            diag[:, col(h)] = mm(p, v_ref[:, col(h)], NN)
    mask_copy.wait()
    spread(m_loc, m_own, x_own, x_loc, 0)

    with jax.named_scope("raw"):
        total_sq = jnp.zeros((BLOCK, DH), F32)
        total_gr = jnp.zeros((BLOCK, DH), F32)
        for h in range(HEADS):
            raw = (
                diag[:, col(h)] + mm(q_ref[:, col(h)] * before, x_loc[h], NN)
            ).astype(BF16).astype(F32)
            diag[:, col(h)] = raw
            scaled = go_ref[:, col(h)].astype(F32) * gain_ref[:, col(h)]
            total_sq += raw * raw
            total_gr += scaled * raw
    with jax.named_scope("norm"):
        width = HEADS * DH
        inv = 1.0 / jnp.sqrt(jnp.sum(total_sq, axis=1, keepdims=True) / width + EPS)
        cross = jnp.sum(total_gr, axis=1, keepdims=True) * inv / width
        for h in range(HEADS):
            normed = diag[:, col(h)] * inv
            scaled = go_ref[:, col(h)].astype(F32) * gain_ref[:, col(h)]
            out_ref[:, col(h)] = (normed * gain_ref[:, col(h)]).astype(BF16)
            d = ((scaled - normed * cross) * inv).astype(BF16)
            d_ref[:, col(h)] = d
            n_loc[h] = mm(q_ref[:, col(h)] * starts, d, TN).astype(BF16)
    with jax.named_scope("start_scatter"):
        start_scatter(n_loc, n_own, 1)

    with jax.named_scope("bdiag"):
        for h in range(HEADS):
            d = d_ref[:, col(h)]
            gp = (mm(d, v_ref[:, col(h)], NT) * weight).astype(BF16)
            gq_ref[:, col(h)] = (
                mm(gp, k_ref[:, col(h)], NN) + mm(d * before, x_loc[h], NT)
            ).astype(BF16)
            acc_k[:, col(h)] = mm(gp, q_ref[:, col(h)], TN)
            acc_v[:, col(h)] = mm(probs[h], d, TN)
    spread(n_loc, n_own, y_own, y_loc, 1)
    with jax.named_scope("final"):
        for h in range(HEADS):
            y = y_loc[h]
            gk_ref[:, col(h)] = (acc_k[:, col(h)] + mm(v_ref[:, col(h)] * after, y, NT)).astype(BF16)
            gv_ref[:, col(h)] = (acc_v[:, col(h)] + mm(k_ref[:, col(h)] * after, y, NN)).astype(BF16)


def store(*refs):
    sems = refs[8]
    copies = [pltpu.make_async_copy(refs[n], refs[4 + n], sems.at[n]) for n in range(4)]
    for copy in copies:
        copy.start()
    for copy in copies:
        copy.wait()


def local(queries, keys, values, grad_out, gain, lengths, block_mask):
    shape = queries.shape
    vmem = pl.BlockSpec(memory_space=pltpu.VMEM)
    hbm = pl.BlockSpec(memory_space=pltpu.HBM)
    square = (HEADS, DH, DH)
    dma = pltpu.SemaphoreType.DMA
    results = pl.pallas_call(
        kernel,
        out_shape=[jax.ShapeDtypeStruct(shape, BF16)] * 4,
        in_specs=[hbm] * 7,
        out_specs=[vmem] * 4,
        scratch_shapes=[pltpu.SMEM((4,), jnp.int32), pltpu.SMEM((2, 6), jnp.int32)]
        + [pltpu.VMEM(shape, BF16)] * 4
        + [
            pltpu.VMEM((1, shape[1]), F32),
            dma((7,)),
            pltpu.VMEM((16, DH), F32),
            pltpu.VMEM((2, 16, DH), F32),
            pltpu.VMEM(square, BF16),
            pltpu.VMEM((8, DH), BF16),
            pltpu.VMEM(shape, F32),
            pltpu.VMEM(shape, F32),
            pltpu.VMEM(shape, F32),
            pltpu.VMEM(shape, BF16),
        ]
        + [pltpu.VMEM(square, BF16)] * 8
        + [
            pltpu.VMEM((2, DH, DH), F32),
            pltpu.VMEM((2, NX, DH, DH), F32),
            pltpu.VMEM((2, DH, DH), F32),
            pltpu.VMEM((2, NY, DH, DH), F32),
            pltpu.VMEM((2, DH, DH), F32),
            dma((2, CHUNKS)),
            dma((2, CHUNKS)),
            dma((2, CHUNKS)),
            dma((2, CHUNKS)),
            dma((2, CHUNKS)),
            dma((2, CHUNKS)),
            dma((2, CHUNKS)),
            dma((2, CHUNKS)),
            dma,
            dma,
        ],
        compiler_params=pltpu.CompilerParams(
            collective_id=0, has_side_effects=True, vmem_limit_bytes=40 * 1024 * 1024
        ),
    )(
        *(
            pltpu.with_memory_space_constraint(a, pltpu.HBM)
            for a in (lengths, block_mask, queries, keys, values, grad_out, gain.reshape(1, -1))
        )
    )
    return pl.pallas_call(
        store,
        out_shape=[jax.ShapeDtypeStruct(shape, BF16)] * 4,
        in_specs=[vmem] * 4,
        out_specs=[hbm] * 4,
        scratch_shapes=[dma((4,))],
    )(*(pltpu.with_memory_space_constraint(r, pltpu.VMEM) for r in results))


def solution(mesh):
    torus = Mesh(mesh.devices.reshape(NY, NX, NC, NZ), TOKEN_AXES)
    tokens = P(TOKEN_AXES, None)
    in_specs = (tokens,) * 4 + (P(), P(), P(TOKEN_AXES[:3], None))
    return jax.shard_map(
        local, mesh=torus, in_specs=in_specs, out_specs=(tokens,) * 4, check_vma=False
    )
```

```python
import jax
import jax.numpy as jnp
from jax import lax
from jax.experimental import pallas as pl
from jax.experimental.pallas import tpu as pltpu
from jax.sharding import Mesh
from jax.sharding import PartitionSpec as P

HEADS = 16
DH = 128
GROUP = 512
BLOCK = 128
EPS = 1e-06
F32 = jnp.float32
BF16 = jnp.bfloat16
TOKEN_AXES = ("cy", "cx", "cc", "head")
NY, NX, NC, NZ = 4, 4, 2, 8
CHIP = NC * NZ
MESH_ID = pl.DeviceIdType.MESH
SIZES = (16,) * 8
LAG = 2
ORDER = (4, 3, 5, 2, 6, 1, 7, 0)
CHUNKS = len(SIZES)
FIRST = [sum(SIZES[:c]) for c in range(CHUNKS)]


def mm(a, b, dims):
    return lax.dot_general(a, b, (dims, ((), ())), preferred_element_type=F32)


NN = ((1,), (0,))
NT = ((1,), (1,))
TN = ((0,), (0,))


def kernel(
    lengths_hbm, mask_hbm, q_hbm, k_hbm, v_hbm, go_hbm, gain_hbm,
    out_ref, gq_ref, k_ref, v_ref, acc_k, acc_v, y_out, after_out,
    lengths, block_mask, q_ref, go_ref, gain_ref, in_sems,
    mask_mine, mask_all, probs, diag, d_ref,
    m_loc, m_own, x_own, x_loc, n_loc, n_own, y_own, y_loc,
    tot_x, rec_x, tot_y, rec_y, entering,
    a_send, a_recv, b_send, b_recv, x_send, x_recv, y_send, y_recv, mask_send, mask_recv,
):
    iy, ix, ic, iz = (lax.axis_index(a) for a in TOKEN_AXES)
    chip = iy * NX + ix
    mine = ic * NZ + iz
    owner = iz * NC + ic
    base = chip * (CHIP * BLOCK)
    start = base + mine * BLOCK

    loads = [
        pltpu.make_async_copy(src, dst, in_sems.at[n])
        for n, (src, dst) in enumerate(
            (
                (k_hbm, k_ref),
                (v_hbm, v_ref),
                (lengths_hbm, lengths),
                (mask_hbm, block_mask),
                (q_hbm, q_ref),
                (gain_hbm, gain_ref),
                (go_hbm, go_ref),
            )
        )
    ]
    for load in loads:
        load.start()

    barrier = pltpu.get_barrier_semaphore()

    def peer(step):
        z = lax.rem(iz + step // NC, NZ)
        c = lax.rem(ic + step, NC)
        return z * NC + c, {"head": z, "cc": c}

    def greet(step, carry):
        pl.semaphore_signal(barrier, 1, device_id=peer(step)[1], device_id_type=MESH_ID)
        return carry

    lax.fori_loop(1, CHIP, greet, 0)
    for step in range(1, NX):
        pl.semaphore_signal(
            barrier, 1, device_id={"cx": lax.rem(ix + step, NX)}, device_id_type=MESH_ID
        )
    for step in range(1, NY):
        pl.semaphore_signal(
            barrier, 1, device_id={"cy": lax.rem(iy + step, NY)}, device_id_type=MESH_ID
        )

    loads[2].wait()
    loads[3].wait()
    b1 = lengths[0]
    b2 = b1 + lengths[1]
    b3 = b2 + lengths[2]

    def seg(p):
        return (
            (p >= b1).astype(jnp.int32) + (p >= b2).astype(jnp.int32) + (p >= b3).astype(jnp.int32)
        )

    def same(a, b):
        return (a == b).astype(F32)

    for g in range(2):
        for n in range(6):
            mask_mine[8 * g + n : 8 * g + n + 1, :] = jnp.full(
                (1, DH), block_mask[g, n].astype(F32), F32
            )

    rows = lax.broadcasted_iota(jnp.int32, (BLOCK, BLOCK), 0)
    cols = lax.broadcasted_iota(jnp.int32, (BLOCK, BLOCK), 1)
    seg_r = seg(start + rows)
    seg_c = seg(start + cols)
    weight = jnp.where((seg_r == seg_c) & (cols <= rows), 1.0, 0.0).astype(F32)
    ends = jnp.where(seg_r == seg(start + BLOCK - 1), 1.0, 0.0).astype(BF16)
    starts = jnp.where(seg_r == seg(start), 1.0, 0.0).astype(BF16)
    before = jnp.where(seg_r == seg(start - 1), 1.0, 0.0).astype(BF16)

    def col(h):
        return slice(h * DH, (h + 1) * DH)

    with jax.named_scope("load_kv"):
        loads[0].wait()
        loads[1].wait()
    with jax.named_scope("make_m"):
        for h in range(HEADS):
            m_loc[h] = mm(k_ref[:, col(h)] * ends, v_ref[:, col(h)], TN).astype(BF16)

    with jax.named_scope("barrier"):
        pl.semaphore_wait(barrier, CHIP - 1 + NX - 1 + NY - 1)

    mask_copy = pltpu.make_async_remote_copy(
        src_ref=mask_mine,
        dst_ref=mask_all.at[ic],
        send_sem=mask_send,
        recv_sem=mask_recv,
        device_id={"cc": 1 - ic},
        device_id_type=MESH_ID,
    )
    mask_copy.start()
    mask_all[ic] = mask_mine[...]

    def chunk(c):
        return pl.ds(FIRST[c], SIZES[c])

    def scatter_copy(src, dst, c, step, phase):
        e, to = peer(step)
        return pltpu.make_async_remote_copy(
            src_ref=src.at[e, chunk(c)],
            dst_ref=dst.at[mine, chunk(c)],
            send_sem=a_send.at[phase],
            recv_sem=a_recv.at[phase, c],
            device_id=to,
            device_id_type=MESH_ID,
        )

    def gather_copy(src, dst, c, step, phase):
        e, to = peer(step)
        r = lax.rem(e, NC) * NZ + e // NC
        return pltpu.make_async_remote_copy(
            src_ref=src.at[r, chunk(c)],
            dst_ref=dst.at[owner, chunk(c)],
            send_sem=b_send.at[phase],
            recv_sem=b_recv.at[phase, c],
            device_id=to,
            device_id_type=MESH_ID,
        )

    def start_square(copy, src, dst, c, phase):
        for away in ORDER:
            for other in range(NC):
                if away or other:
                    copy(src, dst, c, away * NC + other, phase).start()

    def start_scatter(src, dst, phase):
        for c in range(CHUNKS):
            start_square(scatter_copy, src, dst, c, phase)
        dst[mine] = src[owner]

    others = pl.ds(0, CHIP - 1)

    def wait_square(src, dst, c, phase, send, recv):
        pltpu.make_async_remote_copy(
            src_ref=src.at[others, chunk(c)],
            dst_ref=dst.at[others, chunk(c)],
            send_sem=send.at[phase],
            recv_sem=recv.at[phase, c],
            device_id=peer(1)[1],
            device_id_type=MESH_ID,
        ).wait_recv()

    def drain_square(src, dst, phase, send, recv):
        pltpu.make_async_remote_copy(
            src_ref=src.at[others],
            dst_ref=dst.at[others],
            send_sem=send.at[phase],
            recv_sem=recv.at[phase, 0],
            device_id=peer(1)[1],
            device_id_type=MESH_ID,
        ).wait_send()

    def drain_line(slots, phase, axis, me, size, send, recv):
        rest = slots.at[phase, pl.ds(0, size - 1)]
        pltpu.make_async_remote_copy(
            src_ref=rest,
            dst_ref=rest,
            send_sem=send.at[phase],
            recv_sem=recv.at[phase, 0],
            device_id={axis: lax.rem(me + 1, size)},
            device_id_type=MESH_ID,
        ).wait_send()

    def start_gather(src, dst, c, phase):
        start_square(gather_copy, src, dst, c, phase)
        if c == CHUNKS - 1:
            dst[owner] = src[mine]

    def send_line(total, slots, c, phase, axis, me, size, send, recv):
        for step in range(1, size):
            pltpu.make_async_remote_copy(
                src_ref=total.at[phase, chunk(c)],
                dst_ref=slots.at[phase, me, chunk(c)],
                send_sem=send.at[phase],
                recv_sem=recv.at[phase, c],
                device_id={axis: lax.rem(me + size - step, size)},
                device_id_type=MESH_ID,
            ).start()
        slots[phase, me, chunk(c)] = total[phase, chunk(c)]

    def wait_line(slots, c, phase, axis, me, size, send, recv):
        rest = slots.at[phase, pl.ds(0, size - 1), chunk(c)]
        pltpu.make_async_remote_copy(
            src_ref=rest,
            dst_ref=rest,
            send_sem=send.at[phase],
            recv_sem=recv.at[phase, c],
            device_id={axis: lax.rem(me + 1, size)},
            device_id_type=MESH_ID,
        ).wait_recv()

    chip_len = CHIP * BLOCK
    row_len = NX * chip_len
    row_at = iy * row_len
    along_x = ("cx", ix, NX, x_send, x_recv)
    along_y = ("cy", iy, NY, y_send, y_recv)

    def marks(phase):
        forward = phase == 0
        lo = [base + r * BLOCK for r in range(CHIP)]
        edge = [seg(p + BLOCK - 1) if forward else seg(p) for p in lo]
        want = [seg(p - 1) if forward else seg(p + BLOCK) for p in lo]
        enter = seg(base - 1) if forward else seg(base + chip_len)
        return forward, edge, want, enter

    def edge_of(forward, at, size):
        return seg(at + size - 1) if forward else seg(at)

    def stage_x(own, c, phase):
        forward, edge, _, _ = marks(phase)
        last = CHIP - 1 if forward else 0
        total = own[last, chunk(c)].astype(F32)
        for r in range(CHIP):
            if r != last:
                total += same(edge[r], edge[last]) * own[r, chunk(c)].astype(F32)
        tot_x[phase, chunk(c)] = total
        send_line(tot_x, rec_x, c, phase, *along_x)

    def stage_y(c, phase):
        forward, _, _, enter = marks(phase)
        wait_line(rec_x, c, phase, *along_x)
        row_edge = edge_of(forward, row_at, row_len)
        row_total = jnp.zeros((SIZES[c], DH), F32)
        partial = jnp.zeros((SIZES[c], DH), F32)
        for x in range(NX):
            part = rec_x[phase, x, chunk(c)]
            its = edge_of(forward, row_at + x * chip_len, chip_len)
            row_total += same(its, row_edge) * part
            passed = (x < ix) if forward else (x > ix)
            partial += same(its, enter) * passed.astype(F32) * part
        tot_y[phase, chunk(c)] = row_total
        send_line(tot_y, rec_y, c, phase, *along_y)
        entering[phase, chunk(c)] = partial

    def stage_out(own, result, c, phase):
        forward, edge, want, enter = marks(phase)
        wait_line(rec_y, c, phase, *along_y)
        state = entering[phase, chunk(c)]
        for y in range(NY):
            its = edge_of(forward, y * row_len, row_len)
            passed = (y < iy) if forward else (y > iy)
            state += same(its, enter) * passed.astype(F32) * rec_y[phase, y, chunk(c)]

        def block(r):
            return own[r, chunk(c)].astype(F32)

        groups = range(CHIP // 4)
        reach = enter
        for g in groups if forward else reversed(groups):
            inner = range(4) if forward else (3, 2, 1, 0)
            seen = []
            for i in inner:
                r = 4 * g + i
                value = same(reach, want[r]) * state
                for j in seen:
                    hi, lo = (i, j) if forward else (j, i)
                    slot = 8 * (g % 2) + hi * (hi - 1) // 2 + lo
                    pair = mask_all[g // 2, slot : slot + 1, :] * same(edge[4 * g + j], want[r])
                    value += pair * block(4 * g + j)
                result[r, chunk(c)] = value.astype(BF16)
                seen.append(i)
            far = 4 * g + (3 if forward else 0)
            state = same(reach, edge[far]) * state
            for i in inner:
                state += same(edge[4 * g + i], edge[far]) * block(4 * g + i)
            reach = edge[far]

    def spread(loc, own, result, back, phase, filler):
        def first(c):
            with jax.named_scope("wait_scatter"):
                wait_square(loc, own, c, phase, a_send, a_recv)
            with jax.named_scope("stage_x"):
                stage_x(own, c, phase)

        def second(c):
            with jax.named_scope("stage_y"):
                stage_y(c, phase)

        def third(c):
            with jax.named_scope("stage_out"):
                stage_out(own, result, c, phase)
            with jax.named_scope("start_gather"):
                start_gather(result, back, c, phase)

        for s in range(CHUNKS + 2 * LAG):
            if s < CHUNKS:
                first(s)
            if 0 <= s - LAG < CHUNKS:
                second(s - LAG)
            if 0 <= s - 2 * LAG < CHUNKS:
                third(s - 2 * LAG)
            if s < 4:
                with jax.named_scope("filler"):
                    for h in range(4 * s, 4 * s + 4):
                        filler(h)
        for c in range(CHUNKS):
            with jax.named_scope("wait_gather"):
                wait_square(result, back, c, phase, b_send, b_recv)

    with jax.named_scope("start_scatter"):
        start_scatter(m_loc, m_own, 0)
    for load in loads[4:]:
        load.wait()
    def forward_head(h):
        p = (mm(q_ref[:, col(h)], k_ref[:, col(h)], NT) * weight).astype(BF16)
        probs[h] = p
        diag[:, col(h)] = mm(p, v_ref[:, col(h)], NN)

    mask_copy.wait()
    spread(m_loc, m_own, x_own, x_loc, 0, forward_head)

    with jax.named_scope("raw"):
        total_sq = jnp.zeros((BLOCK, DH), F32)
        total_gr = jnp.zeros((BLOCK, DH), F32)
        for h in range(HEADS):
            raw = (
                diag[:, col(h)] + mm(q_ref[:, col(h)] * before, x_loc[h], NN)
            ).astype(BF16).astype(F32)
            diag[:, col(h)] = raw
            scaled = go_ref[:, col(h)].astype(F32) * gain_ref[:, col(h)]
            total_sq += raw * raw
            total_gr += scaled * raw
    with jax.named_scope("norm"):
        width = HEADS * DH
        inv = 1.0 / jnp.sqrt(jnp.sum(total_sq, axis=1, keepdims=True) / width + EPS)
        cross = jnp.sum(total_gr, axis=1, keepdims=True) * inv / width
        for h in range(HEADS):
            normed = diag[:, col(h)] * inv
            scaled = go_ref[:, col(h)].astype(F32) * gain_ref[:, col(h)]
            d = ((scaled - normed * cross) * inv).astype(BF16)
            d_ref[:, col(h)] = d
            n_loc[h] = mm(q_ref[:, col(h)] * starts, d, TN).astype(BF16)
    with jax.named_scope("start_scatter"):
        start_scatter(n_loc, n_own, 1)

    def backward_head(h):
        d = d_ref[:, col(h)]
        out_ref[:, col(h)] = (diag[:, col(h)] * inv * gain_ref[:, col(h)]).astype(BF16)
        gp = (mm(d, v_ref[:, col(h)], NT) * weight).astype(BF16)
        gq_ref[:, col(h)] = (
            mm(gp, k_ref[:, col(h)], NN) + mm(d * before, x_loc[h], NT)
        ).astype(BF16)
        acc_k[:, col(h)] = mm(gp, q_ref[:, col(h)], TN)
        acc_v[:, col(h)] = mm(probs[h], d, TN)

    spread(n_loc, n_own, y_own, y_loc, 1, backward_head)
    drain_square(m_loc, m_own, 0, a_send, a_recv)
    drain_square(x_own, x_loc, 0, b_send, b_recv)
    drain_square(n_loc, n_own, 1, a_send, a_recv)
    drain_square(y_own, y_loc, 1, b_send, b_recv)
    for phase in range(2):
        drain_line(rec_x, phase, *along_x)
        drain_line(rec_y, phase, *along_y)
    after_out[...] = jnp.where(seg_r == seg(start + BLOCK), 1.0, 0.0).astype(BF16)
    y_out[...] = y_loc[...]


def finish(
    out_ref, gq_ref, k_ref, v_ref, acc_k, acc_v, y_ref, after_ref,
    out_hbm, gq_hbm, gk_hbm, gv_hbm,
    gk_ref, gv_ref, sems,
):
    early = [
        pltpu.make_async_copy(out_ref, out_hbm, sems.at[0]),
        pltpu.make_async_copy(gq_ref, gq_hbm, sems.at[1]),
    ]
    for copy in early:
        copy.start()
    after = after_ref[...]
    for h in range(HEADS):
        at = slice(h * DH, (h + 1) * DH)
        gv_ref[:, at] = (acc_v[:, at] + mm(k_ref[:, at] * after, y_ref[h], NN)).astype(BF16)
    late = [
        pltpu.make_async_copy(gv_ref, gv_hbm, sems.at[2]),
        pltpu.make_async_copy(gk_ref, gk_hbm, sems.at[3]),
    ]
    late[0].start()
    for h in range(HEADS):
        at = slice(h * DH, (h + 1) * DH)
        gk_ref[:, at] = (acc_k[:, at] + mm(v_ref[:, at] * after, y_ref[h], NT)).astype(BF16)
    late[1].start()
    for copy in early + late:
        copy.wait()


def local(queries, keys, values, grad_out, gain, lengths, block_mask):
    shape = queries.shape
    vmem = pl.BlockSpec(memory_space=pltpu.VMEM)
    hbm = pl.BlockSpec(memory_space=pltpu.HBM)
    square = (HEADS, DH, DH)
    dma = pltpu.SemaphoreType.DMA
    tokens = jax.ShapeDtypeStruct(shape, BF16)
    sums = jax.ShapeDtypeStruct(shape, F32)
    results = pl.pallas_call(
        kernel,
        out_shape=[tokens] * 4
        + [sums] * 2
        + [jax.ShapeDtypeStruct(square, BF16), jax.ShapeDtypeStruct((BLOCK, DH), BF16)],
        in_specs=[hbm] * 7,
        out_specs=[vmem] * 8,
        scratch_shapes=[
            pltpu.SMEM((4,), jnp.int32),
            pltpu.SMEM((2, 6), jnp.int32),
            pltpu.VMEM(shape, BF16),
            pltpu.VMEM(shape, BF16),
            pltpu.VMEM((1, shape[1]), F32),
            dma((7,)),
            pltpu.VMEM((16, DH), F32),
            pltpu.VMEM((2, 16, DH), F32),
            pltpu.VMEM(square, BF16),
            pltpu.VMEM(shape, F32),
            pltpu.VMEM(shape, BF16),
        ]
        + [pltpu.VMEM(square, BF16)] * 8
        + [
            pltpu.VMEM((2, DH, DH), F32),
            pltpu.VMEM((2, NX, DH, DH), F32),
            pltpu.VMEM((2, DH, DH), F32),
            pltpu.VMEM((2, NY, DH, DH), F32),
            pltpu.VMEM((2, DH, DH), F32),
        ]
        + [dma((2,)), dma((2, CHUNKS))] * 4
        + [dma, dma],
        compiler_params=pltpu.CompilerParams(
            collective_id=0, has_side_effects=True, vmem_limit_bytes=24 * 1024 * 1024
        ),
    )(
        *(
            pltpu.with_memory_space_constraint(a, pltpu.HBM)
            for a in (lengths, block_mask, queries, keys, values, grad_out, gain.reshape(1, -1))
        )
    )
    return pl.pallas_call(
        finish,
        out_shape=[tokens] * 4,
        in_specs=[vmem] * 8,
        out_specs=[hbm] * 4,
        scratch_shapes=[pltpu.VMEM(shape, BF16), pltpu.VMEM(shape, BF16), dma((4,))],
        compiler_params=pltpu.CompilerParams(vmem_limit_bytes=16 * 1024 * 1024),
    )(*(pltpu.with_memory_space_constraint(r, pltpu.VMEM) for r in results))


def solution(mesh):
    torus = Mesh(mesh.devices.reshape(NY, NX, NC, NZ), TOKEN_AXES)
    tokens = P(TOKEN_AXES, None)
    in_specs = (tokens,) * 4 + (P(), P(), P(TOKEN_AXES[:3], None))
    return jax.shard_map(
        local, mesh=torus, in_specs=in_specs, out_specs=(tokens,) * 4, check_vma=False
    )
```

```python
import jax
import jax.numpy as jnp
from jax import lax
from jax.experimental import pallas as pl
from jax.experimental.pallas import tpu as pltpu
from jax.sharding import Mesh
from jax.sharding import PartitionSpec as P

HEADS = 16
DH = 128
GROUP = 512
BLOCK = 128
EPS = 1e-06
F32 = jnp.float32
BF16 = jnp.bfloat16
TOKEN_AXES = ("cy", "cx", "cc", "head")
NY, NX, NC, NZ = 4, 4, 2, 8
CHIP = NC * NZ
MESH_ID = pl.DeviceIdType.MESH
SIZES = (16,) * 8
LAG = 2
EARLY = False
ORDER = (4, 3, 5, 2, 6, 1, 7, 0)
CHUNKS = len(SIZES)
FIRST = [sum(SIZES[:c]) for c in range(CHUNKS)]


def mm(a, b, dims):
    return lax.dot_general(a, b, (dims, ((), ())), preferred_element_type=F32)


NN = ((1,), (0,))
NT = ((1,), (1,))
TN = ((0,), (0,))


def kernel(
    lengths_hbm, mask_hbm, q_hbm, k_hbm, v_hbm, go_hbm, gain_hbm,
    out_ref, gq_ref, k_ref, v_ref, acc_k, acc_v, y_out, after_out,
    lengths, block_mask, q_ref, go_ref, gain_ref, in_sems,
    mask_mine, mask_all, probs, diag, d_ref,
    m_loc, m_own, x_own, x_loc, n_loc, n_own, y_own, y_loc,
    tot_x, rec_x, tot_y, rec_y, entering,
    a_send, a_recv, b_send, b_recv, x_send, x_recv, y_send, y_recv, mask_send, mask_recv,
):
    iy, ix, ic, iz = (lax.axis_index(a) for a in TOKEN_AXES)
    chip = iy * NX + ix
    mine = ic * NZ + iz
    owner = iz * NC + ic
    base = chip * (CHIP * BLOCK)
    start = base + mine * BLOCK

    loads = [
        pltpu.make_async_copy(src, dst, in_sems.at[n])
        for n, (src, dst) in enumerate(
            (
                (k_hbm, k_ref),
                (v_hbm, v_ref),
                (lengths_hbm, lengths),
                (mask_hbm, block_mask),
                (q_hbm, q_ref),
                (gain_hbm, gain_ref),
                (go_hbm, go_ref),
            )
        )
    ]
    for load in loads:
        load.start()

    barrier = pltpu.get_barrier_semaphore()

    def peer(step):
        z = lax.rem(iz + step // NC, NZ)
        c = lax.rem(ic + step, NC)
        return z * NC + c, {"head": z, "cc": c}

    for away in ORDER:
        for other in range(NC):
            if away or other:
                pl.semaphore_signal(
                    barrier, 1, device_id=peer(away * NC + other)[1], device_id_type=MESH_ID
                )
    for step in range(1, NX):
        pl.semaphore_signal(
            barrier, 1, device_id={"cx": lax.rem(ix + step, NX)}, device_id_type=MESH_ID
        )
    for step in range(1, NY):
        pl.semaphore_signal(
            barrier, 1, device_id={"cy": lax.rem(iy + step, NY)}, device_id_type=MESH_ID
        )

    loads[2].wait()
    b1 = lengths[0]
    b2 = b1 + lengths[1]
    b3 = b2 + lengths[2]

    def seg(p):
        return (
            (p >= b1).astype(jnp.int32) + (p >= b2).astype(jnp.int32) + (p >= b3).astype(jnp.int32)
        )

    def same(a, b):
        return (a == b).astype(F32)

    rows = lax.broadcasted_iota(jnp.int32, (BLOCK, BLOCK), 0)
    cols = lax.broadcasted_iota(jnp.int32, (BLOCK, BLOCK), 1)
    seg_r = seg(start + rows)
    seg_c = seg(start + cols)
    weight = jnp.where((seg_r == seg_c) & (cols <= rows), 1.0, 0.0).astype(F32)
    ends = jnp.where(seg_r == seg(start + BLOCK - 1), 1.0, 0.0).astype(BF16)
    starts = jnp.where(seg_r == seg(start), 1.0, 0.0).astype(BF16)
    before = jnp.where(seg_r == seg(start - 1), 1.0, 0.0).astype(BF16)

    def col(h):
        return slice(h * DH, (h + 1) * DH)

    with jax.named_scope("load_kv"):
        loads[0].wait()
        loads[1].wait()
    with jax.named_scope("make_m"):
        for h in range(HEADS):
            m_loc[h] = mm(k_ref[:, col(h)] * ends, v_ref[:, col(h)], TN).astype(BF16)

    with jax.named_scope("barrier"):
        pl.semaphore_wait(barrier, CHIP - 1 + NX - 1 + NY - 1)

    def chunk(c):
        return pl.ds(FIRST[c], SIZES[c])

    def scatter_copy(src, dst, c, step, phase):
        e, to = peer(step)
        return pltpu.make_async_remote_copy(
            src_ref=src.at[e, chunk(c)],
            dst_ref=dst.at[mine, chunk(c)],
            send_sem=a_send.at[phase],
            recv_sem=a_recv.at[phase, c],
            device_id=to,
            device_id_type=MESH_ID,
        )

    def gather_copy(src, dst, c, step, phase):
        e, to = peer(step)
        r = lax.rem(e, NC) * NZ + e // NC
        return pltpu.make_async_remote_copy(
            src_ref=src.at[r, chunk(c)],
            dst_ref=dst.at[owner, chunk(c)],
            send_sem=b_send.at[phase],
            recv_sem=b_recv.at[phase, c],
            device_id=to,
            device_id_type=MESH_ID,
        )

    def start_square(copy, src, dst, c, phase):
        for away in ORDER:
            for other in range(NC):
                if away or other:
                    copy(src, dst, c, away * NC + other, phase).start()

    def start_scatter(src, dst, phase):
        for c in range(CHUNKS):
            start_square(scatter_copy, src, dst, c, phase)
        dst[mine] = src[owner]

    others = pl.ds(0, CHIP - 1)

    def wait_square(src, dst, c, phase, send, recv):
        pltpu.make_async_remote_copy(
            src_ref=src.at[others, chunk(c)],
            dst_ref=dst.at[others, chunk(c)],
            send_sem=send.at[phase],
            recv_sem=recv.at[phase, c],
            device_id=peer(1)[1],
            device_id_type=MESH_ID,
        ).wait_recv()

    def drain_square(src, dst, phase, send, recv):
        pltpu.make_async_remote_copy(
            src_ref=src.at[others],
            dst_ref=dst.at[others],
            send_sem=send.at[phase],
            recv_sem=recv.at[phase, 0],
            device_id=peer(1)[1],
            device_id_type=MESH_ID,
        ).wait_send()

    def drain_line(slots, phase, axis, me, size, send, recv):
        rest = slots.at[phase, pl.ds(0, size - 1)]
        pltpu.make_async_remote_copy(
            src_ref=rest,
            dst_ref=rest,
            send_sem=send.at[phase],
            recv_sem=recv.at[phase, 0],
            device_id={axis: lax.rem(me + 1, size)},
            device_id_type=MESH_ID,
        ).wait_send()

    def start_gather(src, dst, c, phase):
        start_square(gather_copy, src, dst, c, phase)
        if c == CHUNKS - 1:
            dst[owner] = src[mine]

    def send_line(total, slots, c, phase, axis, me, size, send, recv):
        for step in range(1, size):
            pltpu.make_async_remote_copy(
                src_ref=total.at[phase, chunk(c)],
                dst_ref=slots.at[phase, me, chunk(c)],
                send_sem=send.at[phase],
                recv_sem=recv.at[phase, c],
                device_id={axis: lax.rem(me + size - step, size)},
                device_id_type=MESH_ID,
            ).start()
        slots[phase, me, chunk(c)] = total[phase, chunk(c)]

    def wait_line(slots, c, phase, axis, me, size, send, recv):
        rest = slots.at[phase, pl.ds(0, size - 1), chunk(c)]
        pltpu.make_async_remote_copy(
            src_ref=rest,
            dst_ref=rest,
            send_sem=send.at[phase],
            recv_sem=recv.at[phase, c],
            device_id={axis: lax.rem(me + 1, size)},
            device_id_type=MESH_ID,
        ).wait_recv()

    chip_len = CHIP * BLOCK
    row_len = NX * chip_len
    row_at = iy * row_len
    along_x = ("cx", ix, NX, x_send, x_recv)
    along_y = ("cy", iy, NY, y_send, y_recv)

    def marks(phase):
        forward = phase == 0
        lo = [base + r * BLOCK for r in range(CHIP)]
        edge = [seg(p + BLOCK - 1) if forward else seg(p) for p in lo]
        want = [seg(p - 1) if forward else seg(p + BLOCK) for p in lo]
        enter = seg(base - 1) if forward else seg(base + chip_len)
        return forward, edge, want, enter

    def edge_of(forward, at, size):
        return seg(at + size - 1) if forward else seg(at)

    def stage_x(own, c, phase):
        forward, edge, _, _ = marks(phase)
        last = CHIP - 1 if forward else 0
        total = own[last, chunk(c)].astype(F32)
        for r in range(CHIP):
            if r != last:
                total += same(edge[r], edge[last]) * own[r, chunk(c)].astype(F32)
        tot_x[phase, chunk(c)] = total
        send_line(tot_x, rec_x, c, phase, *along_x)

    def stage_y(c, phase):
        forward, _, _, enter = marks(phase)
        wait_line(rec_x, c, phase, *along_x)
        row_edge = edge_of(forward, row_at, row_len)
        row_total = jnp.zeros((SIZES[c], DH), F32)
        partial = jnp.zeros((SIZES[c], DH), F32)
        for x in range(NX):
            part = rec_x[phase, x, chunk(c)]
            its = edge_of(forward, row_at + x * chip_len, chip_len)
            row_total += same(its, row_edge) * part
            passed = (x < ix) if forward else (x > ix)
            partial += same(its, enter) * passed.astype(F32) * part
        tot_y[phase, chunk(c)] = row_total
        send_line(tot_y, rec_y, c, phase, *along_y)
        entering[phase, chunk(c)] = partial

    def stage_out(own, result, c, phase):
        forward, edge, want, enter = marks(phase)
        wait_line(rec_y, c, phase, *along_y)
        state = entering[phase, chunk(c)]
        for y in range(NY):
            its = edge_of(forward, y * row_len, row_len)
            passed = (y < iy) if forward else (y > iy)
            state += same(its, enter) * passed.astype(F32) * rec_y[phase, y, chunk(c)]

        def block(r):
            return own[r, chunk(c)].astype(F32)

        groups = range(CHIP // 4)
        reach = enter
        for g in groups if forward else reversed(groups):
            inner = range(4) if forward else (3, 2, 1, 0)
            seen = []
            for i in inner:
                r = 4 * g + i
                value = same(reach, want[r]) * state
                for j in seen:
                    hi, lo = (i, j) if forward else (j, i)
                    slot = 8 * (g % 2) + hi * (hi - 1) // 2 + lo
                    pair = mask_all[g // 2, slot : slot + 1, :] * same(edge[4 * g + j], want[r])
                    value += pair * block(4 * g + j)
                result[r, chunk(c)] = value.astype(BF16)
                seen.append(i)
            far = 4 * g + (3 if forward else 0)
            state = same(reach, edge[far]) * state
            for i in inner:
                state += same(edge[4 * g + i], edge[far]) * block(4 * g + i)
            reach = edge[far]

    def spread(loc, own, result, back, phase, filler):
        def first(c):
            with jax.named_scope("wait_scatter"):
                wait_square(loc, own, c, phase, a_send, a_recv)
            with jax.named_scope("stage_x"):
                stage_x(own, c, phase)

        def second(c):
            with jax.named_scope("stage_y"):
                stage_y(c, phase)

        def third(c):
            with jax.named_scope("stage_out"):
                stage_out(own, result, c, phase)
            with jax.named_scope("start_gather"):
                start_gather(result, back, c, phase)

        for s in range(CHUNKS + 2 * LAG):
            if EARLY and 0 <= s - LAG < CHUNKS:
                second(s - LAG)
            if s < CHUNKS:
                first(s)
            if not EARLY and 0 <= s - LAG < CHUNKS:
                second(s - LAG)
            if 0 <= s - 2 * LAG < CHUNKS:
                third(s - 2 * LAG)
            if s < 4:
                with jax.named_scope("filler"):
                    for h in range(4 * s, 4 * s + 4):
                        filler(h)
        for c in range(CHUNKS):
            with jax.named_scope("wait_gather"):
                wait_square(result, back, c, phase, b_send, b_recv)

    with jax.named_scope("start_scatter"):
        start_scatter(m_loc, m_own, 0)
    for load in loads[3:]:
        load.wait()
    for g in range(2):
        for n in range(6):
            mask_mine[8 * g + n : 8 * g + n + 1, :] = jnp.full(
                (1, DH), block_mask[g, n].astype(F32), F32
            )
    def forward_head(h):
        p = (mm(q_ref[:, col(h)], k_ref[:, col(h)], NT) * weight).astype(BF16)
        probs[h] = p
        diag[:, col(h)] = mm(p, v_ref[:, col(h)], NN)

    mask_copy = pltpu.make_async_remote_copy(
        src_ref=mask_mine,
        dst_ref=mask_all.at[ic],
        send_sem=mask_send,
        recv_sem=mask_recv,
        device_id={"cc": 1 - ic},
        device_id_type=MESH_ID,
    )
    mask_copy.start()
    mask_all[ic] = mask_mine[...]
    mask_copy.wait()
    spread(m_loc, m_own, x_own, x_loc, 0, forward_head)

    with jax.named_scope("raw"):
        total_sq = jnp.zeros((BLOCK, DH), F32)
        total_gr = jnp.zeros((BLOCK, DH), F32)
        for h in range(HEADS):
            raw = (
                diag[:, col(h)] + mm(q_ref[:, col(h)] * before, x_loc[h], NN)
            ).astype(BF16).astype(F32)
            diag[:, col(h)] = raw
            scaled = go_ref[:, col(h)].astype(F32) * gain_ref[:, col(h)]
            total_sq += raw * raw
            total_gr += scaled * raw
    with jax.named_scope("norm"):
        width = HEADS * DH
        inv = 1.0 / jnp.sqrt(jnp.sum(total_sq, axis=1, keepdims=True) / width + EPS)
        cross = jnp.sum(total_gr, axis=1, keepdims=True) * inv / width
        for h in range(HEADS):
            normed = diag[:, col(h)] * inv
            scaled = go_ref[:, col(h)].astype(F32) * gain_ref[:, col(h)]
            d = ((scaled - normed * cross) * inv).astype(BF16)
            d_ref[:, col(h)] = d
            n_loc[h] = mm(q_ref[:, col(h)] * starts, d, TN).astype(BF16)
    with jax.named_scope("start_scatter"):
        start_scatter(n_loc, n_own, 1)

    def backward_head(h):
        d = d_ref[:, col(h)]
        out_ref[:, col(h)] = (diag[:, col(h)] * inv * gain_ref[:, col(h)]).astype(BF16)
        gp = (mm(d, v_ref[:, col(h)], NT) * weight).astype(BF16)
        gq_ref[:, col(h)] = (
            mm(gp, k_ref[:, col(h)], NN) + mm(d * before, x_loc[h], NT)
        ).astype(BF16)
        acc_k[:, col(h)] = mm(gp, q_ref[:, col(h)], TN)
        acc_v[:, col(h)] = mm(probs[h], d, TN)

    spread(n_loc, n_own, y_own, y_loc, 1, backward_head)
    drain_square(m_loc, m_own, 0, a_send, a_recv)
    drain_square(x_own, x_loc, 0, b_send, b_recv)
    drain_square(n_loc, n_own, 1, a_send, a_recv)
    drain_square(y_own, y_loc, 1, b_send, b_recv)
    for phase in range(2):
        drain_line(rec_x, phase, *along_x)
        drain_line(rec_y, phase, *along_y)
    after_out[...] = jnp.where(seg_r == seg(start + BLOCK), 1.0, 0.0).astype(BF16)
    y_out[...] = y_loc[...]


def finish(
    out_ref, gq_ref, k_ref, v_ref, acc_k, acc_v, y_ref, after_ref,
    out_hbm, gq_hbm, gk_hbm, gv_hbm,
    gk_ref, gv_ref, sems,
):
    early = [
        pltpu.make_async_copy(out_ref, out_hbm, sems.at[0]),
        pltpu.make_async_copy(gq_ref, gq_hbm, sems.at[1]),
    ]
    for copy in early:
        copy.start()
    after = after_ref[...]
    for h in range(HEADS):
        at = slice(h * DH, (h + 1) * DH)
        gv_ref[:, at] = (acc_v[:, at] + mm(k_ref[:, at] * after, y_ref[h], NN)).astype(BF16)
    late = [
        pltpu.make_async_copy(gv_ref, gv_hbm, sems.at[2]),
        pltpu.make_async_copy(gk_ref, gk_hbm, sems.at[3]),
    ]
    late[0].start()
    for h in range(HEADS):
        at = slice(h * DH, (h + 1) * DH)
        gk_ref[:, at] = (acc_k[:, at] + mm(v_ref[:, at] * after, y_ref[h], NT)).astype(BF16)
    late[1].start()
    for copy in early + late:
        copy.wait()


def local(queries, keys, values, grad_out, gain, lengths, block_mask):
    shape = queries.shape
    vmem = pl.BlockSpec(memory_space=pltpu.VMEM)
    hbm = pl.BlockSpec(memory_space=pltpu.HBM)
    square = (HEADS, DH, DH)
    dma = pltpu.SemaphoreType.DMA
    tokens = jax.ShapeDtypeStruct(shape, BF16)
    sums = jax.ShapeDtypeStruct(shape, F32)
    results = pl.pallas_call(
        kernel,
        out_shape=[tokens] * 4
        + [sums] * 2
        + [jax.ShapeDtypeStruct(square, BF16), jax.ShapeDtypeStruct((BLOCK, DH), BF16)],
        in_specs=[hbm] * 7,
        out_specs=[vmem] * 8,
        scratch_shapes=[
            pltpu.SMEM((4,), jnp.int32),
            pltpu.SMEM((2, 6), jnp.int32),
            pltpu.VMEM(shape, BF16),
            pltpu.VMEM(shape, BF16),
            pltpu.VMEM((1, shape[1]), F32),
            dma((7,)),
            pltpu.VMEM((16, DH), F32),
            pltpu.VMEM((2, 16, DH), F32),
            pltpu.VMEM(square, BF16),
            pltpu.VMEM(shape, F32),
            pltpu.VMEM(shape, BF16),
        ]
        + [pltpu.VMEM(square, BF16)] * 8
        + [
            pltpu.VMEM((2, DH, DH), F32),
            pltpu.VMEM((2, NX, DH, DH), F32),
            pltpu.VMEM((2, DH, DH), F32),
            pltpu.VMEM((2, NY, DH, DH), F32),
            pltpu.VMEM((2, DH, DH), F32),
        ]
        + [dma((2,)), dma((2, CHUNKS))] * 4
        + [dma, dma],
        compiler_params=pltpu.CompilerParams(
            collective_id=0, has_side_effects=True, vmem_limit_bytes=24 * 1024 * 1024
        ),
    )(
        *(
            pltpu.with_memory_space_constraint(a, pltpu.HBM)
            for a in (lengths, block_mask, queries, keys, values, grad_out, gain.reshape(1, -1))
        )
    )
    return pl.pallas_call(
        finish,
        out_shape=[tokens] * 4,
        in_specs=[vmem] * 8,
        out_specs=[hbm] * 4,
        scratch_shapes=[pltpu.VMEM(shape, BF16), pltpu.VMEM(shape, BF16), dma((4,))],
        compiler_params=pltpu.CompilerParams(vmem_limit_bytes=16 * 1024 * 1024),
    )(*(pltpu.with_memory_space_constraint(r, pltpu.VMEM) for r in results))


def solution(mesh):
    torus = Mesh(mesh.devices.reshape(NY, NX, NC, NZ), TOKEN_AXES)
    tokens = P(TOKEN_AXES, None)
    in_specs = (tokens,) * 4 + (P(), P(), P(TOKEN_AXES[:3], None))
    return jax.shard_map(
        local, mesh=torus, in_specs=in_specs, out_specs=(tokens,) * 4, check_vma=False
    )
```
